32 devices in a mesh: dp: 2 (over y), expert: 4 (over x, core), tensor: 4 (over z).
Axes of the slice: x: 2, y: 2, z: 4, core: 2. Of those that a mesh axis runs over, the one named last changes fastest.
Arguments:
- hidden_rows: bfloat16 [128, 7168], P(('dp', 'expert')), may hold values from -6 to 6
- expert_ids: int32 [128, 8], P(('dp', 'expert')), may hold values from 0 to 15, all different within a row; in each aligned block of 16 rows (0 to 15, 16 to 31, ...) at most 16 rows name the same one
- route_weights: float32 [128, 8], P(('dp', 'expert')), may hold values from 0.1 to 1
- w_gate: bfloat16 [16, 1024, 7168], P(('expert', 'tensor'), 'dp'), may hold values from -0.0625 to 0.0625
- w_up: bfloat16 [16, 1024, 7168], P(('expert', 'tensor'), 'dp'), may hold values from -0.0625 to 0.0625
- w_down: bfloat16 [16, 1024, 7168], P(('expert', 'tensor'), 'dp'), may hold values from -0.1875 to 0.1875
Outputs:
- moe_out: bfloat16 [128, 7168], P(('dp', 'expert'))
The draws below stay inside these ranges and needn't reach their ends.
Inputs may be any that keep to these rules, and one draw needn't show every extreme that they name: `expert_ids`: each row names 8 different experts. Within the 16 rows of one attention group (one index of dp+expert), no expert is named by more than 16 rows, a bound that some block reaches.
All inputs are finite; a program needn't handle non-finite values.
Results may differ from the reference program's by a relative error of at most 0.0057.
Values may be sent and summed in bfloat16 or wider, within the bound.
A program may use at most 64 MiB of HBM per device.

```python
import math
import jax
import jax.numpy as jnp
import numpy as np
from jax import lax

D = 7168
FF = 1024
TOP = 8
GROUP_ROWS = 16
EXPERTS = 16
CAP = 16
ROWS = 128


def block_scale(rng, shape, shards, least, top_value):
    gain, own = 1.0, jax.random.fold_in(rng, 6)
    for position, parts in shards:
        heights = jnp.exp(jax.random.uniform(jax.random.fold_in(own, position), (parts,), jnp.float32, least / len(shards), top_value / len(shards)))
        gain = gain * jnp.repeat(heights, shape[position] // parts).reshape([-1 if axis == position else 1 for axis in range(len(shape))])
    return gain


def deal_out(stream_key, own, number, rows, number_of, top, most, lean):
    order = jax.random.permutation(stream_key, number_of)
    crowded, ordinary = portions_of(number_of, rows * top, most, lean, True), portions_of(number_of, rows * top, most, lean, False)
    places = jnp.arange(number_of)

    def named(lengths, rotation):
        used = int((lengths > 0).sum())
        fixed = max(1, used // 4)
        shifted = fixed + (places - fixed + rotation * (used - fixed)) % max(1, number_of - fixed)
        return jnp.zeros((number_of,), jnp.int32).at[order[jnp.where(places < fixed, places, shifted)]].set(jnp.asarray(lengths, jnp.int32))

    lengths = jnp.where(number % 4 == 0, named(crowded, number // 4), named(ordinary, number - number // 4 - 1))
    mixed = jax.random.permutation(jax.random.fold_in(own, 3), number_of)
    source_of, receiver = mixed[0:number_of // 2 * 2:2], mixed[1:number_of // 2 * 2:2]
    margin = jnp.minimum(lengths[source_of] - 1, most - lengths[receiver]) // 2
    margin = jnp.where((source_of == order[0]) | (receiver == order[0]) | (lengths[receiver] == 0), 0, jnp.maximum(margin, 0))
    shifted = jax.random.randint(jax.random.fold_in(own, 4), (number_of // 2,), 0, 1 << 20) % (margin + 1)
    lengths = lengths.at[source_of].add(-shifted).at[receiver].add(shifted)
    items = jnp.searchsorted(jnp.cumsum(lengths), jnp.arange(rows * top), side="right").astype(jnp.int32)
    table = items.reshape(top, rows).T
    table = table[jax.random.permutation(jax.random.fold_in(own, 1), rows)]
    rotation = jax.random.randint(jax.random.fold_in(own, 2), (rows, 1), 0, top)
    return jnp.take_along_axis(table, (jnp.arange(top)[None, :] + rotation) % top, axis=1)


def portions_of(number_of, total, bound, lean, full):
    portions = [(1 << 20) // math.isqrt(grade ** lean) + 1 for grade in range(1, number_of + 1)]
    largest = bound if full else min(bound, max(-(-total // number_of), total * portions[0] // sum(portions)))
    least = 1 if total - largest >= number_of - 1 else 0
    given, spare = [largest] + [least] * (number_of - 1), total - largest - least * (number_of - 1)
    while spare > 0:
        movable = [i for i in range(1, number_of) if given[i] < largest] or [i for i in range(1, number_of) if given[i] < bound]
        mass, remaining = sum([portions[i] for i in movable]), spare
        for i in movable:
            more = min(bound - given[i], max(1, remaining * portions[i] // mass), spare)
            given[i] = given[i] + more
            spare = spare - more
    return np.array(given)


def gaussian(own_key, shape, width, bound, pieces=(), kind=jnp.bfloat16):
    array = jax.random.normal(own_key, shape, jnp.float32) * width
    if len(pieces) > 0:
        array = block_scale(own_key, shape, pieces, -0.22, 0.18) * array
    return jnp.clip(array, min=-bound, max=bound).astype(kind)


def setup_inputs(seed: int = 0) -> dict:
    splits = jax.random.split(jax.random.key(seed), 7)
    hidden_rows = gaussian(splits[0], (ROWS, D), 1.0, 6.0, ((0, 8),))
    expert_ids_keys = jax.random.split(jax.random.fold_in(splits[1], 1), ROWS // GROUP_ROWS)
    expert_ids_turns = jax.random.permutation(jax.random.fold_in(splits[1], 3), ROWS // GROUP_ROWS)
    expert_ids = jax.vmap(lambda own, number: deal_out(jax.random.fold_in(splits[1], 2), own, number, GROUP_ROWS, EXPERTS, TOP, CAP, 2))(expert_ids_keys, expert_ids_turns).reshape((ROWS, TOP))
    route_weights = jnp.clip(0.1 + 0.9 * jax.random.uniform(splits[2], (ROWS, TOP), jnp.float32) ** block_scale(splits[2], (ROWS, TOP), ((0, 8),), -0.2, 0.2), 0.1, 1.0)
    w_gate = gaussian(splits[3], (EXPERTS, FF, D), D ** -0.5, 0.0625, ((0, 16), (1, 2)))
    w_up = gaussian(splits[4], (EXPERTS, FF, D), D ** -0.5, 0.0625, ((0, 16), (1, 2)))
    w_down = gaussian(splits[5], (EXPERTS, FF, D), FF ** -0.5, 0.1875, ((0, 16), (1, 2)))
    return dict(hidden_rows=hidden_rows, expert_ids=expert_ids, route_weights=route_weights, w_gate=w_gate, w_up=w_up, w_down=w_down)


def slot_table(route_ids, targets, capacity):
    matches = jnp.any(route_ids[:, :, None] == targets[None, None, :], axis=1)
    positions = jnp.cumsum(matches.astype(jnp.int32), axis=0) - 1
    slot_numbers = jnp.arange(capacity, dtype=jnp.int32)
    slot_hits = matches[:, :, None] & (positions[:, :, None] == slot_numbers[None, None, :])
    return jnp.transpose(slot_hits, (1, 2, 0)).astype(jnp.float32)


def route_share(route_ids, route_weights, targets):
    chosen = (route_ids[:, :, None] == targets[None, None, :]).astype(jnp.float32)
    return jnp.sum(route_weights[:, :, None] * chosen, axis=1)


def reference(hidden_rows, expert_ids, route_weights, w_gate, w_up, w_down):
    group_count = hidden_rows.shape[0] // GROUP_ROWS
    group_data = hidden_rows.reshape(group_count, GROUP_ROWS, D).astype(jnp.float32)
    group_ids = expert_ids.reshape(group_count, GROUP_ROWS, TOP)
    group_weights = route_weights.reshape(group_count, GROUP_ROWS, TOP)

    def one_expert(mixed_rows, expert_index):
        own_target = jnp.reshape(expert_index, (1,)).astype(jnp.int32)

        def group_table(route_ids):
            return slot_table(route_ids, own_target, CAP)[0]

        def group_share(route_ids, weights_row):
            return route_share(route_ids, weights_row, own_target)[:, 0]

        tables = jax.vmap(group_table)(group_ids)
        slot_rows = jnp.einsum("gcr,grd->gcd", tables, group_data, precision=lax.Precision.HIGHEST)
        slot_rows = slot_rows.reshape(group_count * CAP, D).astype(jnp.bfloat16)
        gate_value = jnp.dot(slot_rows, jnp.transpose(w_gate[expert_index]), preferred_element_type=jnp.float32)
        up_value = jnp.dot(slot_rows, jnp.transpose(w_up[expert_index]), preferred_element_type=jnp.float32)
        activation = (jax.nn.silu(gate_value) * up_value).astype(jnp.bfloat16)
        expert_out = jnp.dot(activation, w_down[expert_index], preferred_element_type=jnp.float32).astype(jnp.bfloat16)
        expert_out = expert_out.reshape(group_count, CAP, D).astype(jnp.float32)
        shares = jax.vmap(group_share)(group_ids, group_weights)
        coefficient = tables * shares[:, None, :]
        mixed_rows = mixed_rows + jnp.einsum("gcr,gcd->grd", coefficient, expert_out, precision=lax.Precision.HIGHEST)
        return mixed_rows, None

    start_rows = jnp.zeros((group_count, GROUP_ROWS, D), jnp.float32)
    mixed_rows, _ = lax.scan(one_expert, start_rows, jnp.arange(EXPERTS, dtype=jnp.int32))
    return mixed_rows.reshape(group_count * GROUP_ROWS, D).astype(jnp.bfloat16)
```

```python
import functools

import jax
import jax.numpy as jnp
from jax import lax
from jax.experimental import pallas as pl
from jax.experimental.pallas import tpu as pltpu
from jax.sharding import PartitionSpec as P


def slot_table(route_ids, targets, capacity):
    matches = jnp.any(route_ids[:, :, None] == targets[None, None, :], axis=1)
    positions = jnp.cumsum(matches.astype(jnp.int32), axis=0) - 1
    slot_numbers = jnp.arange(capacity, dtype=jnp.int32)
    slot_hits = matches[:, :, None] & (positions[:, :, None] == slot_numbers[None, None, :])
    return jnp.transpose(slot_hits, (1, 2, 0)).astype(jnp.float32)


def route_share(route_ids, route_weights, targets):
    chosen = (route_ids[:, :, None] == targets[None, None, :]).astype(jnp.float32)
    return jnp.sum(route_weights[:, :, None] * chosen, axis=1)


def row_product(left, right):
    return lax.dot_general(
        left, right, (((1,), (1,)), ((), ())), preferred_element_type=jnp.float32
    )


def general_body(hidden_rows, expert_ids, route_weights, w_gate, w_up, w_down):
    expert_count = lax.axis_size("expert")
    tensor_count = lax.axis_size("tensor")
    lane_index = lax.axis_index("tensor")
    group_rows, feature_width = hidden_rows.shape
    chosen_count = expert_ids.shape[1]
    experts_all = expert_count * tensor_count
    capacity = min(group_rows, max(2, 2 * group_rows * chosen_count // experts_all))
    targets = jnp.arange(expert_count, dtype=jnp.int32) * tensor_count + lane_index
    own_table = slot_table(expert_ids, targets, capacity)
    all_rows, all_ids = (
        lax.all_gather(hidden_rows, "expert", axis=0, tiled=True),
        lax.all_gather(expert_ids, "expert", axis=0, tiled=True),
    )
    own_expert = lax.axis_index("expert") * tensor_count + lane_index
    own_target = jnp.reshape(own_expert, (1,))

    def group_table(route_ids):
        return slot_table(route_ids, own_target, capacity)[0]

    tables = jax.vmap(group_table)(all_ids.reshape(expert_count, group_rows, chosen_count))
    arrived = jnp.einsum(
        "gcr,grd->gcd",
        tables.astype(jnp.bfloat16),
        all_rows.reshape(expert_count, group_rows, feature_width),
        preferred_element_type=jnp.float32,
    ).astype(jnp.bfloat16)
    gate_weight = w_gate[0]
    up_weight = w_up[0]
    down_weight = w_down[0]
    block_piece = lax.all_gather(arrived, "dp", axis=0, tiled=True)
    row_count = block_piece.shape[0]
    activate_row_count = block_piece.shape[0]
    flat_rows = block_piece.reshape(activate_row_count * capacity, feature_width)
    gate_value = row_product(flat_rows, gate_weight)
    up_value = row_product(flat_rows, up_weight)
    activation = (jax.nn.silu(gate_value) * up_value).astype(jnp.bfloat16)
    down_part = jnp.dot(activation, down_weight, preferred_element_type=jnp.float32)
    partial_value = down_part.reshape(row_count, capacity, feature_width)
    summed = lax.psum_scatter(partial_value, "dp", scatter_dimension=0, tiled=True)
    expert_out = summed.astype(jnp.bfloat16)
    back_rows = lax.all_to_all(expert_out, "expert", split_axis=0, concat_axis=0, tiled=True)
    route_table = route_share(expert_ids, route_weights, targets)
    coefficient = own_table * jnp.transpose(route_table)[:, None, :]
    mixed_rows = jnp.einsum(
        "gcr,gcd->rd", coefficient, back_rows.astype(jnp.float32), precision=lax.Precision.HIGHEST
    )
    summed_rows = lax.psum(mixed_rows, "tensor")
    return summed_rows.astype(jnp.bfloat16)


def split_count(width, unit, most):
    units = width // unit
    return max(n for n in range(1, most + 1) if units % n == 0)


def split_rounds(width, count):
    units = width // 128
    edges = [-(-units * i // count) * 128 for i in range(count + 1)]
    return tuple((low, high - low) for low, high in zip(edges, edges[1:]))


def fused_kernel(
    sizes, rounds, plan,
    hid, ids, wts, wg, wu, wd, out,
    rows_all, wg_v, wu_v, wd_v, gate_acc, up_acc, act, table,
    pair_send, pair_recv, part, a_send, a_recv, b_send, b_recv, c_send, c_recv, f_send, own_total,
    ids_v, wts_v, own_sem, id_sem, w_sem, wd_sem, g_recv, sent_sem, t_recv, pa_recv, aa_recv, ba_recv, ca_recv,
    fa_recv, o_sem,
):
    dp_count, expert_count, tensor_count, chunks = sizes
    depth, gather_times, return_times = plan
    group, width = hid.shape
    chunk = width // chunks
    half = width // 2
    quarter = half // tensor_count
    block = 2 * group
    y, e, z = lax.axis_index("dp"), lax.axis_index("expert"), lax.axis_index("tensor")
    x, c = e // 2, e % 2
    xe, ce, yy = e + 2 - 4 * x, e + 1 - 2 * c, 1 - y
    cxe = ce + 2 - 4 * x

    def device(dp, expert, tensor):
        return {"dp": dp, "expert": expert, "tensor": tensor}

    def number(dp, expert):
        return dp * expert_count + expert

    def rows_of(g):
        return pl.ds(pl.multiple_of(g * group, group), group)

    def cols_of(j):
        return slice(j * chunk, (j + 1) * chunk)

    def remote(src, dst, send, recv, target):
        return pltpu.make_async_remote_copy(
            src_ref=src, dst_ref=dst, send_sem=send, recv_sem=recv,
            device_id=target, device_id_type=pl.DeviceIdType.MESH,
        )

    def in_order(table):
        return sorted((start + step * k, n, k) for n, (count, start, step) in enumerate(table) for k in range(count))

    own = number(y, e)
    own_copy = pltpu.make_async_copy(hid, rows_all.at[rows_of(own), :], own_sem)
    own_copy.start()
    id_copies = [
        pltpu.make_async_copy(ids, ids_v, id_sem.at[0]), pltpu.make_async_copy(wts, wts_v, id_sem.at[1])
    ]
    for copy in id_copies:
        copy.start()

    plane = [
        (p, device((y + p // expert_count) % dp_count, (e + p % expert_count) % expert_count, z))
        for p in range(1, dp_count * expert_count)
    ]
    line = [
        (d, o, device(y, e if o == 0 else ce, (z + d) % tensor_count))
        for d in range(tensor_count) for o in range(2)
    ]
    barrier = pltpu.get_barrier_semaphore()
    greeted = [t for _, t in plane] + [t for d, _, t in line if d > 0]
    for target in greeted:
        pl.semaphore_signal(barrier, inc=1, device_id=target, device_id_type=pl.DeviceIdType.MESH)

    def weight_copy(which, j):
        src, dst = ((wg, wg_v), (wu, wu_v), (wd, wd_v))[which]
        sem = wd_sem if which == 2 else w_sem.at[j]
        return pltpu.make_async_copy(src.at[0, :, cols_of(j)], dst.at[:, cols_of(j)], sem)

    to_x, to_y, to_pair = device(y, xe, z), device(yy, e, z), device(y, ce, z)
    g_x, g_y, g_d = number(y, xe), number(yy, e), number(yy, xe)
    g_sent, t_sent, p_sent, a_sent, b_sent, c_sent, f_sent = (sent_sem.at[n] for n in range(7))

    def piece(g, j):
        return rows_all.at[rows_of(g), cols_of(j)]

    def forward(kind, g, j, target):
        return remote(piece(g, j), piece(g, j), g_sent, g_recv.at[min(kind, 3), j], target)

    def own_send(kind, j):
        return remote(piece(own, j), piece(own, j), g_sent, g_recv.at[kind, j], (to_x, to_y, None, to_pair)[kind])

    def diagonal(j):
        return forward(2, g_x, j, to_y) if j % 2 == 0 else forward(2, g_y, j, to_x)

    own_copy.wait()
    pl.semaphore_wait(barrier, len(greeted))
    for j in range(depth):
        for kind in (0, 1, 3):
            own_send(kind, j).start()
    for j in range(chunks):
        weight_copy(0, j).start()
        weight_copy(1, j).start()
    for j in range(chunks):
        weight_copy(2, j).start()

    table_copies = [
        remote(table.at[rows_of(own), :], table.at[rows_of(own), :], t_sent, t_recv, target) for _, target in plane
    ]

    def share_table(_):
        for copy in id_copies:
            copy.wait()
        expert_rows = lax.broadcasted_iota(jnp.int32, (table.shape[1], group), 0)
        share = jnp.zeros((table.shape[1], group), jnp.float32)
        for k in range(ids_v.shape[0]):
            share = share + jnp.where(ids_v[k : k + 1, :] == expert_rows, wts_v[k : k + 1, :], 0.0)
        same = lax.broadcasted_iota(jnp.int32, (group, group), 0) == lax.broadcasted_iota(jnp.int32, (group, group), 1)
        table[rows_of(own), :] = lax.dot_general(
            same.astype(jnp.float32), share, (((1,), (1,)), ((), ())),
            precision=lax.Precision.HIGHEST, preferred_element_type=jnp.float32,
        )
        for copy in table_copies:
            copy.start()

    def relay(s):
        later = s + depth < chunks
        forward(0, g_x, s, to_x).wait_recv()
        if s % 2 == 0:
            diagonal(s).start()
        if later:
            own_send(1, s + depth).start()
        forward(4, g_x, s, to_pair).start()
        forward(1, g_y, s, to_y).wait_recv()
        if s % 2 == 1:
            diagonal(s).start()
        if later:
            own_send(0, s + depth).start()
            own_send(3, s + depth).start()
        forward(5, g_y, s, to_pair).start()

    def relay_far(s):
        forward(2, g_d, s, to_y).wait_recv()
        forward(6, g_d, s, to_pair).start()

    def project(acc, weight, j):
        value = row_product(rows_all[:, cols_of(j)], weight[:, cols_of(j)])
        acc[...] = value if j == 0 else acc[...] + value

    def gate(j):
        arrived = rows_all.at[0 : rows_all.shape[0] // 2, cols_of(j)]
        remote(arrived, arrived, g_sent, g_recv.at[3, j], to_pair).wait_recv()
        filled = wg_v.at[:, 0 : 2 * chunk]
        pltpu.make_async_copy(filled, filled, w_sem.at[j]).wait()
        project(gate_acc, wg_v, j)

    def up(j):
        project(up_acc, wu_v, j)

    gather_stages = (relay, relay_far, gate, up, share_table)
    for _, n, k in in_order(gather_times):
        gather_stages[n](k)
    act[...] = (jax.nn.silu(gate_acc[...]) * up_acc[...]).astype(act.dtype)

    others = table.at[0 : len(plane) * group, :]
    remote(others, others, t_sent, t_recv, to_pair).wait_recv()
    lane_all = lax.broadcasted_iota(jnp.int32, table.shape, 1)
    coef = jnp.sum(
        jnp.where(lane_all == e * tensor_count + z, table[...], 0.0), axis=1, keepdims=True
    )
    pltpu.make_async_copy(wd_v, wd_v, wd_sem).wait()

    a, b = x + c * (y - x), y + c * (x - y)
    to_a = device(y + c * (1 - 2 * y), e + (1 - c) * (xe - e), z)
    to_b = device(y + (1 - c) * (1 - 2 * y), e + c * (xe - e), z)

    def block_rows(s, u):
        return pl.ds(pl.multiple_of((s * (1 + c) + u * (2 - c)) * block, block), block)

    steps = [(i, r) for r in range(len(rounds)) for i in range(tensor_count)]

    def span(k):
        i, r = steps[k]
        return slice(i * quarter + rounds[r][0], i * quarter + rounds[r][0] + rounds[r][1])

    def place(h, q, r):
        return pl.ds(pl.multiple_of(h * half + q * quarter + rounds[r][0], 128), rounds[r][1])

    def pair_copy(k):
        return remote(pair_send.at[:, span(k)], pair_recv.at[:, span(k)], p_sent, pa_recv.at[k], to_pair)

    def a_copy(k):
        return remote(a_send.at[:, :, span(k)], a_recv.at[:, :, span(k)], a_sent, aa_recv.at[k], to_a)

    def b_copy(k):
        return remote(b_send.at[:, span(k)], b_recv.at[:, span(k)], b_sent, ba_recv.at[k], to_b)

    def c_copy(k):
        i, r = steps[k]
        return remote(c_send.at[:, span(k)], c_recv.at[:, span(k)], c_sent, ca_recv.at[r],
                      device(y, e, (z + 1 + i) % tensor_count))

    def f_copy(o, r, target):
        rows = rows_of(c if o == 0 else 1 - c)
        place_r = slice(rounds[r][0], rounds[r][0] + rounds[r][1])
        return remote(f_send.at[rows, place_r], out.at[:, place(c, z, r)], f_sent, fa_recv, target)

    def compute(k):
        i, r = steps[k]
        q = (z + 1 + i) % tensor_count
        away = jnp.dot(act[...], wd_v[:, place(1 - c, q, r)], preferred_element_type=jnp.float32)
        pair_send[:, span(k)] = (away * coef).astype(pair_send.dtype)
        pair_copy(k).start()
        kept = jnp.dot(act[...], wd_v[:, place(c, q, r)], preferred_element_type=jnp.float32)
        part[:, span(k)] = kept * coef

    def both(s, u, k):
        rows = block_rows(s, u)
        return part[rows, span(k)] + pair_recv[rows, span(k)].astype(jnp.float32)

    def stage_a(k):
        pair_copy(k).wait_recv()
        for u in range(2):
            a_send[u, :, span(k)] = both(1 - a, u, k).astype(a_send.dtype)
        a_copy(k).start()

    def stage_b(k):
        a_copy(k).wait_recv()
        total = both(a, 1 - b, k) + a_recv[1 - b, :, span(k)].astype(jnp.float32)
        b_send[:, span(k)] = total.astype(b_send.dtype)
        b_copy(k).start()

    def stage_c(k):
        i, r = steps[k]
        b_copy(k).wait_recv()
        total = both(a, b, k) + a_recv[b, :, span(k)].astype(jnp.float32)
        total = total + b_recv[:, span(k)].astype(jnp.float32)
        if i < tensor_count - 1:
            c_send[:, span(k)] = total.astype(c_send.dtype)
            c_copy(k).start()
            return
        own_total[:, rounds[r][0] : rounds[r][0] + rounds[r][1]] = total

    def stage_f(r):
        low, size = rounds[r]
        place_r = slice(low, low + size)
        filled = c_recv.at[:, 0 : (tensor_count - 1) * size]
        remote(filled, filled, c_sent, ca_recv.at[r], to_pair).wait_recv()
        total = own_total[:, place_r]
        for other in range(tensor_count - 1):
            total = total + c_recv[:, span(r * tensor_count + other)].astype(jnp.float32)
        f_send[:, place_r] = total.astype(f_send.dtype)
        for _, o, target in reversed(line[1:]):
            f_copy(o, r, target).start()
        pltpu.make_async_copy(f_send.at[rows_of(c), place_r], out.at[:, place(c, z, r)], o_sem).start()

    return_stages = (compute, stage_a, stage_b, stage_c, stage_f)
    for _, n, k in in_order(return_times):
        return_stages[n](k)

    def sent(ref, sem):
        remote(ref, ref, sem, t_recv, to_pair).wait_send()

    sent(rows_all.at[0 : 7 * group, :], g_sent)
    sent(others, t_sent)
    sent(pair_send, p_sent)
    sent(a_send, a_sent)
    sent(b_send, b_sent)
    sent(c_send.at[:, 0 : (tensor_count - 1) * quarter], c_sent)
    from_others = out.at[:, 0 : width - quarter]
    sent(from_others, f_sent)
    remote(from_others, from_others, f_sent, fa_recv, to_pair).wait_recv()
    kept_rows = out.at[:, 0:quarter]
    pltpu.make_async_copy(kept_rows, kept_rows, o_sem).wait()


def fused_body(shape, hidden_rows, expert_ids, route_weights, w_gate, w_up, w_down):
    dp_count, expert_count, tensor_count = shape["dp"], shape["expert"], shape["tensor"]
    group, width = hidden_rows.shape
    hidden = w_gate.shape[1]
    rows = dp_count * expert_count * group
    half = width // 2
    quarter = half // tensor_count
    chunks = split_count(width, 256, 7)
    rounds = split_rounds(quarter, 1)
    count = len(rounds) * tensor_count
    lanes = -(-expert_count * tensor_count // 128) * 128
    gather_times = (
        (chunks, 2.4, 0.85), (chunks, 5.1, 0.8), (chunks, 6.1, 0.8), (chunks, 6.45, 0.8), (1, 7.55, 0.0),
    )
    return_times = (
        (count, 0.0, 0.62), (count, 1.6, 0.62), (count, 5.0, 1.6), (count, 8.6, 1.4), (len(rounds), 15.0, 5.0),
    )
    dma = pltpu.SemaphoreType.DMA
    bf16, f32 = jnp.bfloat16, jnp.float32
    any_space = pl.BlockSpec(memory_space=pl.ANY)
    scratch = [
        pltpu.VMEM((rows, width), bf16),
        pltpu.VMEM((hidden, width), bf16),
        pltpu.VMEM((hidden, width), bf16),
        pltpu.VMEM((hidden, width), bf16),
        pltpu.VMEM((rows, hidden), f32),
        pltpu.VMEM((rows, hidden), f32),
        pltpu.VMEM((rows, hidden), bf16),
        pltpu.VMEM((rows, lanes), f32),
        pltpu.VMEM((rows, half), bf16),
        pltpu.VMEM((rows, half), bf16),
        pltpu.VMEM((rows, half), f32),
        pltpu.VMEM((2, 2 * group, half), bf16),
        pltpu.VMEM((2, 2 * group, half), bf16),
        pltpu.VMEM((2 * group, half), bf16),
        pltpu.VMEM((2 * group, half), bf16),
        pltpu.VMEM((2 * group, half), bf16),
        pltpu.VMEM((2 * group, half), bf16),
        pltpu.VMEM((2 * group, quarter), bf16),
        pltpu.VMEM((2 * group, quarter), f32),
        pltpu.VMEM(expert_ids.shape[::-1], expert_ids.dtype),
        pltpu.VMEM(route_weights.shape[::-1], route_weights.dtype),
        dma,
        dma((2,)),
        dma((chunks,)),
        dma,
        dma((4, chunks)),
        dma((7,)),
        dma,
        dma((count,)),
        dma((count,)),
        dma((count,)),
        dma((len(rounds),)),
        dma,
        dma,
    ]
    return pl.pallas_call(
        functools.partial(
            fused_kernel, (dp_count, expert_count, tensor_count, chunks), rounds,
            (4, gather_times, return_times),
        ),
        out_shape=jax.ShapeDtypeStruct((group, width), bf16),
        in_specs=[any_space] * 6,
        out_specs=any_space,
        scratch_shapes=scratch,
        compiler_params=pltpu.CompilerParams(
            collective_id=0, has_side_effects=True, vmem_limit_bytes=60 * 1024 * 1024
        ),
        name="routed_experts",
    )(hidden_rows, expert_ids.T, route_weights.T, w_gate, w_up, w_down)


def body(shape, hidden_rows, expert_ids, route_weights, w_gate, w_up, w_down):
    dp_count, expert_count, tensor_count = shape["dp"], shape["expert"], shape["tensor"]
    group, width = hidden_rows.shape
    chosen = expert_ids.shape[1]
    dense = 2 * group * chosen >= group * expert_count * tensor_count
    square = dp_count == 2 and expert_count == 2 * dp_count
    aligned = width % (256 * tensor_count) == 0 and group % 16 == 0
    chosen_body = general_body
    if dense and square and aligned and tensor_count > 1 and w_gate.shape[0] == 1:
        chosen_body = functools.partial(fused_body, shape)
    return chosen_body(hidden_rows, expert_ids, route_weights, w_gate, w_up, w_down)


def solution(mesh):
    return jax.shard_map(
        functools.partial(body, dict(mesh.shape)),
        mesh=mesh,
        in_specs=(
            P(("dp", "expert"), None),
            P(("dp", "expert"), None),
            P(("dp", "expert"), None),
            P(("expert", "tensor"), "dp", None),
            P(("expert", "tensor"), "dp", None),
            P(("expert", "tensor"), "dp", None),
        ),
        out_specs=P(("dp", "expert"), None),
        check_vma=False,
    )
```

```python
import functools

import jax
import jax.numpy as jnp
from jax import lax
from jax.experimental import pallas as pl
from jax.experimental.pallas import tpu as pltpu
from jax.sharding import PartitionSpec as P


def slot_table(route_ids, targets, capacity):
    matches = jnp.any(route_ids[:, :, None] == targets[None, None, :], axis=1)
    positions = jnp.cumsum(matches.astype(jnp.int32), axis=0) - 1
    slot_numbers = jnp.arange(capacity, dtype=jnp.int32)
    slot_hits = matches[:, :, None] & (positions[:, :, None] == slot_numbers[None, None, :])
    return jnp.transpose(slot_hits, (1, 2, 0)).astype(jnp.float32)


def route_share(route_ids, route_weights, targets):
    chosen = (route_ids[:, :, None] == targets[None, None, :]).astype(jnp.float32)
    return jnp.sum(route_weights[:, :, None] * chosen, axis=1)


def row_product(left, right):
    return lax.dot_general(
        left, right, (((1,), (1,)), ((), ())), preferred_element_type=jnp.float32
    )


def general_body(hidden_rows, expert_ids, route_weights, w_gate, w_up, w_down):
    expert_count = lax.axis_size("expert")
    tensor_count = lax.axis_size("tensor")
    lane_index = lax.axis_index("tensor")
    group_rows, feature_width = hidden_rows.shape
    chosen_count = expert_ids.shape[1]
    experts_all = expert_count * tensor_count
    capacity = min(group_rows, max(2, 2 * group_rows * chosen_count // experts_all))
    targets = jnp.arange(expert_count, dtype=jnp.int32) * tensor_count + lane_index
    own_table = slot_table(expert_ids, targets, capacity)
    all_rows, all_ids = (
        lax.all_gather(hidden_rows, "expert", axis=0, tiled=True),
        lax.all_gather(expert_ids, "expert", axis=0, tiled=True),
    )
    own_expert = lax.axis_index("expert") * tensor_count + lane_index
    own_target = jnp.reshape(own_expert, (1,))

    def group_table(route_ids):
        return slot_table(route_ids, own_target, capacity)[0]

    tables = jax.vmap(group_table)(all_ids.reshape(expert_count, group_rows, chosen_count))
    arrived = jnp.einsum(
        "gcr,grd->gcd",
        tables.astype(jnp.bfloat16),
        all_rows.reshape(expert_count, group_rows, feature_width),
        preferred_element_type=jnp.float32,
    ).astype(jnp.bfloat16)
    gate_weight = w_gate[0]
    up_weight = w_up[0]
    down_weight = w_down[0]
    block_piece = lax.all_gather(arrived, "dp", axis=0, tiled=True)
    row_count = block_piece.shape[0]
    activate_row_count = block_piece.shape[0]
    flat_rows = block_piece.reshape(activate_row_count * capacity, feature_width)
    gate_value = row_product(flat_rows, gate_weight)
    up_value = row_product(flat_rows, up_weight)
    activation = (jax.nn.silu(gate_value) * up_value).astype(jnp.bfloat16)
    down_part = jnp.dot(activation, down_weight, preferred_element_type=jnp.float32)
    partial_value = down_part.reshape(row_count, capacity, feature_width)
    summed = lax.psum_scatter(partial_value, "dp", scatter_dimension=0, tiled=True)
    expert_out = summed.astype(jnp.bfloat16)
    back_rows = lax.all_to_all(expert_out, "expert", split_axis=0, concat_axis=0, tiled=True)
    route_table = route_share(expert_ids, route_weights, targets)
    coefficient = own_table * jnp.transpose(route_table)[:, None, :]
    mixed_rows = jnp.einsum(
        "gcr,gcd->rd", coefficient, back_rows.astype(jnp.float32), precision=lax.Precision.HIGHEST
    )
    summed_rows = lax.psum(mixed_rows, "tensor")
    return summed_rows.astype(jnp.bfloat16)


def split_count(width, unit, most):
    units = width // unit
    return max(n for n in range(1, most + 1) if units % n == 0)


def split_rounds(width, count):
    units = width // 128
    edges = [-(-units * i // count) * 128 for i in range(count + 1)]
    return tuple((low, high - low) for low, high in zip(edges, edges[1:]))


def fused_kernel(
    sizes, rounds, plan,
    hid, ids, wts, wg, wu, wd, out,
    rows_all, wg_v, wu_v, wd_v, gate_acc, up_acc, act, table,
    pair_send, pair_recv, part, a_send, a_recv, b_send, b_recv, c_send, c_recv, f_send, own_total,
    ids_v, wts_v, own_sem, id_sem, w_sem, wd_sem, g_recv, sent_sem, t_recv, pa_recv, aa_recv, ba_recv, ca_recv,
    fa_recv, o_sem,
):
    dp_count, expert_count, tensor_count, chunks = sizes
    depth, gather_times, return_times = plan
    group, width = hid.shape
    chunk = width // chunks
    half = width // 2
    quarter = half // tensor_count
    block = 2 * group
    y, e, z = lax.axis_index("dp"), lax.axis_index("expert"), lax.axis_index("tensor")
    x, c = e // 2, e % 2
    xe, ce, yy = e + 2 - 4 * x, e + 1 - 2 * c, 1 - y
    cxe = ce + 2 - 4 * x

    def device(dp, expert, tensor):
        return {"dp": dp, "expert": expert, "tensor": tensor}

    def number(dp, expert):
        return dp * expert_count + expert

    def rows_of(g):
        return pl.ds(pl.multiple_of(g * group, group), group)

    def cols_of(j):
        return slice(j * chunk, (j + 1) * chunk)

    def remote(src, dst, send, recv, target):
        return pltpu.make_async_remote_copy(
            src_ref=src, dst_ref=dst, send_sem=send, recv_sem=recv,
            device_id=target, device_id_type=pl.DeviceIdType.MESH,
        )

    def in_order(table):
        return sorted((start + step * k, n, k) for n, (count, start, step) in enumerate(table) for k in range(count))

    own = number(y, e)
    own_copy = pltpu.make_async_copy(hid, rows_all.at[rows_of(own), :], own_sem)
    own_copy.start()
    id_copies = [
        pltpu.make_async_copy(ids, ids_v, id_sem.at[0]), pltpu.make_async_copy(wts, wts_v, id_sem.at[1])
    ]
    for copy in id_copies:
        copy.start()

    plane = [
        (p, device((y + p // expert_count) % dp_count, (e + p % expert_count) % expert_count, z))
        for p in range(1, dp_count * expert_count)
    ]
    line = [
        (d, o, device(y, e if o == 0 else ce, (z + d) % tensor_count))
        for d in range(tensor_count) for o in range(2)
    ]
    barrier = pltpu.get_barrier_semaphore()
    greeted = [t for _, t in plane] + [t for d, _, t in line if d > 0]
    for target in greeted:
        pl.semaphore_signal(barrier, inc=1, device_id=target, device_id_type=pl.DeviceIdType.MESH)

    def weight_copy(which, j):
        src, dst = ((wg, wg_v), (wu, wu_v), (wd, wd_v))[which]
        sem = wd_sem if which == 2 else w_sem.at[j]
        return pltpu.make_async_copy(src.at[0, :, cols_of(j)], dst.at[:, cols_of(j)], sem)

    to_x, to_y, to_pair = device(y, xe, z), device(yy, e, z), device(y, ce, z)
    g_x, g_y, g_d = number(y, xe), number(yy, e), number(yy, xe)
    g_sent, t_sent, p_sent, a_sent, b_sent, c_sent, f_sent = (sent_sem.at[n] for n in range(7))

    def piece(g, j):
        return rows_all.at[rows_of(g), cols_of(j)]

    def forward(kind, g, j, target):
        return remote(piece(g, j), piece(g, j), g_sent, g_recv.at[min(kind, 3), j], target)

    def own_send(kind, j):
        return remote(piece(own, j), piece(own, j), g_sent, g_recv.at[kind, j], (to_x, to_y, None, to_pair)[kind])

    def diagonal(j):
        return forward(2, g_x, j, to_y) if j % 2 == 0 else forward(2, g_y, j, to_x)

    own_copy.wait()
    pl.semaphore_wait(barrier, len(greeted))
    for j in range(depth):
        for kind in (0, 1, 3):
            own_send(kind, j).start()
    for j in range(chunks):
        weight_copy(0, j).start()
        weight_copy(1, j).start()
    for j in range(chunks):
        weight_copy(2, j).start()

    table_copies = [
        remote(table.at[rows_of(own), :], table.at[rows_of(own), :], t_sent, t_recv, target) for _, target in plane
    ]

    def share_table(_):
        for copy in id_copies:
            copy.wait()
        expert_rows = lax.broadcasted_iota(jnp.int32, (table.shape[1], group), 0)
        share = jnp.zeros((table.shape[1], group), jnp.float32)
        for k in range(ids_v.shape[0]):
            share = share + jnp.where(ids_v[k : k + 1, :] == expert_rows, wts_v[k : k + 1, :], 0.0)
        same = lax.broadcasted_iota(jnp.int32, (group, group), 0) == lax.broadcasted_iota(jnp.int32, (group, group), 1)
        table[rows_of(own), :] = lax.dot_general(
            same.astype(jnp.float32), share, (((1,), (1,)), ((), ())),
            precision=lax.Precision.HIGHEST, preferred_element_type=jnp.float32,
        )

    def send_table(_):
        for copy in table_copies:
            copy.start()

    def relay(s):
        later = s + depth < chunks
        forward(0, g_x, s, to_x).wait_recv()
        if s % 2 == 0:
            diagonal(s).start()
        if later:
            own_send(1, s + depth).start()
        forward(4, g_x, s, to_pair).start()
        forward(1, g_y, s, to_y).wait_recv()
        if s % 2 == 1:
            diagonal(s).start()
        if later:
            own_send(0, s + depth).start()
            own_send(3, s + depth).start()
        forward(5, g_y, s, to_pair).start()

    def relay_far(s):
        forward(2, g_d, s, to_y).wait_recv()
        forward(6, g_d, s, to_pair).start()

    def project(acc, weight, j):
        value = row_product(rows_all[:, cols_of(j)], weight[:, cols_of(j)])
        acc[...] = value if j == 0 else acc[...] + value

    def gate(j):
        arrived = rows_all.at[0 : rows_all.shape[0] // 2, cols_of(j)]
        remote(arrived, arrived, g_sent, g_recv.at[3, j], to_pair).wait_recv()
        filled = wg_v.at[:, 0 : 2 * chunk]
        pltpu.make_async_copy(filled, filled, w_sem.at[j]).wait()
        project(gate_acc, wg_v, j)

    def up(j):
        project(up_acc, wu_v, j)

    gather_stages = (relay, relay_far, gate, up, send_table, share_table)
    for _, n, k in in_order(gather_times):
        gather_stages[n](k)
    act[...] = (jax.nn.silu(gate_acc[...]) * up_acc[...]).astype(act.dtype)

    others = table.at[0 : len(plane) * group, :]
    remote(others, others, t_sent, t_recv, to_pair).wait_recv()
    lane_all = lax.broadcasted_iota(jnp.int32, table.shape, 1)
    coef = jnp.sum(
        jnp.where(lane_all == e * tensor_count + z, table[...], 0.0), axis=1, keepdims=True
    )
    pltpu.make_async_copy(wd_v, wd_v, wd_sem).wait()

    a, b = x + c * (y - x), y + c * (x - y)
    to_a = device(y + c * (1 - 2 * y), e + (1 - c) * (xe - e), z)
    to_b = device(y + (1 - c) * (1 - 2 * y), e + c * (xe - e), z)

    def block_rows(s, u):
        return pl.ds(pl.multiple_of((s * (1 + c) + u * (2 - c)) * block, block), block)

    steps = [(i, r) for r in range(len(rounds)) for i in range(tensor_count)]

    def span(k):
        i, r = steps[k]
        return slice(i * quarter + rounds[r][0], i * quarter + rounds[r][0] + rounds[r][1])

    def place(h, q, r):
        return pl.ds(pl.multiple_of(h * half + q * quarter + rounds[r][0], 128), rounds[r][1])

    def pair_copy(k):
        return remote(pair_send.at[:, span(k)], pair_recv.at[:, span(k)], p_sent, pa_recv.at[k], to_pair)

    def a_copy(k):
        return remote(a_send.at[:, :, span(k)], a_recv.at[:, :, span(k)], a_sent, aa_recv.at[k], to_a)

    def b_copy(k):
        return remote(b_send.at[:, span(k)], b_recv.at[:, span(k)], b_sent, ba_recv.at[k], to_b)

    def c_copy(k):
        i, r = steps[k]
        return remote(c_send.at[:, span(k)], c_recv.at[:, span(k)], c_sent, ca_recv.at[r],
                      device(y, e, (z + 1 + i) % tensor_count))

    def f_copy(o, r, target):
        rows = rows_of(c if o == 0 else 1 - c)
        place_r = slice(rounds[r][0], rounds[r][0] + rounds[r][1])
        return remote(f_send.at[rows, place_r], out.at[:, place(c, z, r)], f_sent, fa_recv, target)

    def compute(k):
        i, r = steps[k]
        q = (z + 1 + i) % tensor_count
        away = jnp.dot(act[...], wd_v[:, place(1 - c, q, r)], preferred_element_type=jnp.float32)
        pair_send[:, span(k)] = (away * coef).astype(pair_send.dtype)
        pair_copy(k).start()
        kept = jnp.dot(act[...], wd_v[:, place(c, q, r)], preferred_element_type=jnp.float32)
        part[:, span(k)] = kept * coef

    def both(s, u, k):
        rows = block_rows(s, u)
        return part[rows, span(k)] + pair_recv[rows, span(k)].astype(jnp.float32)

    def stage_a(k):
        pair_copy(k).wait_recv()
        for u in range(2):
            a_send[u, :, span(k)] = both(1 - a, u, k).astype(a_send.dtype)
        a_copy(k).start()

    def stage_b(k):
        a_copy(k).wait_recv()
        total = both(a, 1 - b, k) + a_recv[1 - b, :, span(k)].astype(jnp.float32)
        b_send[:, span(k)] = total.astype(b_send.dtype)
        b_copy(k).start()

    def stage_c(k):
        i, r = steps[k]
        b_copy(k).wait_recv()
        total = both(a, b, k) + a_recv[b, :, span(k)].astype(jnp.float32)
        total = total + b_recv[:, span(k)].astype(jnp.float32)
        if i < tensor_count - 1:
            c_send[:, span(k)] = total.astype(c_send.dtype)
            c_copy(k).start()
            return
        own_total[:, rounds[r][0] : rounds[r][0] + rounds[r][1]] = total

    def stage_f(r):
        low, size = rounds[r]
        place_r = slice(low, low + size)
        filled = c_recv.at[:, 0 : (tensor_count - 1) * size]
        remote(filled, filled, c_sent, ca_recv.at[r], to_pair).wait_recv()
        total = own_total[:, place_r]
        for other in range(tensor_count - 1):
            total = total + c_recv[:, span(r * tensor_count + other)].astype(jnp.float32)
        f_send[:, place_r] = total.astype(f_send.dtype)
        for _, o, target in reversed(line[1:]):
            f_copy(o, r, target).start()
        pltpu.make_async_copy(f_send.at[rows_of(c), place_r], out.at[:, place(c, z, r)], o_sem).start()

    return_stages = (compute, stage_a, stage_b, stage_c, stage_f)
    for _, n, k in in_order(return_times):
        return_stages[n](k)

    def sent(ref, sem):
        remote(ref, ref, sem, t_recv, to_pair).wait_send()

    sent(rows_all.at[0 : 7 * group, :], g_sent)
    sent(others, t_sent)
    sent(pair_send, p_sent)
    sent(a_send, a_sent)
    sent(b_send, b_sent)
    sent(c_send.at[:, 0 : (tensor_count - 1) * quarter], c_sent)
    from_others = out.at[:, 0 : width - quarter]
    sent(from_others, f_sent)
    remote(from_others, from_others, f_sent, fa_recv, to_pair).wait_recv()
    kept_rows = out.at[:, 0:quarter]
    pltpu.make_async_copy(kept_rows, kept_rows, o_sem).wait()


def fused_body(shape, hidden_rows, expert_ids, route_weights, w_gate, w_up, w_down):
    dp_count, expert_count, tensor_count = shape["dp"], shape["expert"], shape["tensor"]
    group, width = hidden_rows.shape
    hidden = w_gate.shape[1]
    rows = dp_count * expert_count * group
    half = width // 2
    quarter = half // tensor_count
    chunks = split_count(width, 256, 7)
    rounds = split_rounds(quarter, 2)
    count = len(rounds) * tensor_count
    lanes = -(-expert_count * tensor_count // 128) * 128
    gather_times = (
        (chunks, 2.4, 0.85), (chunks, 5.1, 0.8), (chunks, 6.1, 0.8), (chunks, 6.45, 0.8), (1, 7.55, 0.0),
        (1, 7.54, 0.0),
    )
    return_times = (
        (count, 0, 0.32), (count, 1.0, 0.4), (count, 4.4, 0.8), (count, 7.2, 0.9), (len(rounds), 13.0, 3.0),
    )
    dma = pltpu.SemaphoreType.DMA
    bf16, f32 = jnp.bfloat16, jnp.float32
    any_space = pl.BlockSpec(memory_space=pl.ANY)
    scratch = [
        pltpu.VMEM((rows, width), bf16),
        pltpu.VMEM((hidden, width), bf16),
        pltpu.VMEM((hidden, width), bf16),
        pltpu.VMEM((hidden, width), bf16),
        pltpu.VMEM((rows, hidden), f32),
        pltpu.VMEM((rows, hidden), f32),
        pltpu.VMEM((rows, hidden), bf16),
        pltpu.VMEM((rows, lanes), f32),
        pltpu.VMEM((rows, half), bf16),
        pltpu.VMEM((rows, half), bf16),
        pltpu.VMEM((rows, half), f32),
        pltpu.VMEM((2, 2 * group, half), bf16),
        pltpu.VMEM((2, 2 * group, half), bf16),
        pltpu.VMEM((2 * group, half), bf16),
        pltpu.VMEM((2 * group, half), bf16),
        pltpu.VMEM((2 * group, half), bf16),
        pltpu.VMEM((2 * group, half), bf16),
        pltpu.VMEM((2 * group, quarter), bf16),
        pltpu.VMEM((2 * group, quarter), f32),
        pltpu.VMEM(expert_ids.shape[::-1], expert_ids.dtype),
        pltpu.VMEM(route_weights.shape[::-1], route_weights.dtype),
        dma,
        dma((2,)),
        dma((chunks,)),
        dma,
        dma((4, chunks)),
        dma((7,)),
        dma,
        dma((count,)),
        dma((count,)),
        dma((count,)),
        dma((len(rounds),)),
        dma,
        dma,
    ]
    return pl.pallas_call(
        functools.partial(
            fused_kernel, (dp_count, expert_count, tensor_count, chunks), rounds,
            (4, gather_times, return_times),
        ),
        out_shape=pltpu.VMEM((group, width), bf16),
        in_specs=[any_space] * 6,
        out_specs=pl.BlockSpec(memory_space=pltpu.VMEM),
        scratch_shapes=scratch,
        compiler_params=pltpu.CompilerParams(
            collective_id=0, has_side_effects=True, vmem_limit_bytes=60 * 1024 * 1024
        ),
        name="routed_experts",
    )(hidden_rows, expert_ids.T, route_weights.T, w_gate, w_up, w_down)


def body(shape, hidden_rows, expert_ids, route_weights, w_gate, w_up, w_down):
    dp_count, expert_count, tensor_count = shape["dp"], shape["expert"], shape["tensor"]
    group, width = hidden_rows.shape
    chosen = expert_ids.shape[1]
    dense = 2 * group * chosen >= group * expert_count * tensor_count
    square = dp_count == 2 and expert_count == 2 * dp_count
    aligned = width % (256 * tensor_count) == 0 and group % 16 == 0
    chosen_body = general_body
    if dense and square and aligned and tensor_count > 1 and w_gate.shape[0] == 1:
        chosen_body = functools.partial(fused_body, shape)
    return chosen_body(hidden_rows, expert_ids, route_weights, w_gate, w_up, w_down)


def solution(mesh):
    return jax.shard_map(
        functools.partial(body, dict(mesh.shape)),
        mesh=mesh,
        in_specs=(
            P(("dp", "expert"), None),
            P(("dp", "expert"), None),
            P(("dp", "expert"), None),
            P(("expert", "tensor"), "dp", None),
            P(("expert", "tensor"), "dp", None),
            P(("expert", "tensor"), "dp", None),
        ),
        out_specs=P(("dp", "expert"), None),
        check_vma=False,
    )
```
